32 devices in a mesh: expert: 8 (over y, x, core), dp: 4 (over z).
Axes of the slice: x: 2, y: 2, z: 4, core: 2. Of those that a mesh axis runs over, the one named last changes fastest.
Arguments:
- tokens: bfloat16 [4096, 2048], P(('expert', 'dp')), may hold values from -6 to 6
- cotangent: bfloat16 [4096, 2048], P(('expert', 'dp')), may hold values from -6 to 6
- expert_ids: int32 [4096, 8], P(('expert', 'dp')), may hold values from 0 to 31, all different within a row; in each aligned block of 128 rows (0 to 127, 128 to 255, ...) at most 40 rows name the same one
- combine_weights: float32 [4096, 8], P(('expert', 'dp')), may hold values from 0.1 to 1
- w_gate: bfloat16 [32, 2048, 384], P('expert'), may hold values from -0.125 to 0.125
- w_up: bfloat16 [32, 2048, 384], P('expert'), may hold values from -0.125 to 0.125
- w_down: bfloat16 [32, 2048, 384], P('expert'), may hold values from -0.3125 to 0.3125
- swap_flags: int32 [4], replicated, may hold values 0 or 1
Outputs:
- mixed: bfloat16 [4096, 2048], P(('expert', 'dp'))
- input_grad: bfloat16 [4096, 2048], P(('expert', 'dp'))
- grad_gate: bfloat16 [32, 2048, 384], P('expert', 'dp')
- grad_up: bfloat16 [32, 2048, 384], P('expert', 'dp')
- grad_down: bfloat16 [32, 2048, 384], P('expert', 'dp')
The draws below stay inside these ranges and needn't reach their ends.
Inputs may be any that keep to these rules, and one draw needn't show every extreme that they name: `expert_ids`: in each aligned block of 128 token rows (the rows of one device) no expert is named by more than 40 rows, a bound that some block reaches. `swap_flags`: entry j concerns the pair of expert-axis indices j and j + 4.
All inputs are finite; a program needn't handle non-finite values.
Results may differ from the reference program's by a relative error of at most 0.0095.
Values may be sent and summed in bfloat16 or wider, within the bound.
A program may use at most 192 MiB of HBM per device.

```python
import math
import jax
import jax.numpy as jnp
import numpy as np
from jax import lax

D = 2048
FW = 384
TOPK = 8
EXP_DEV = 4
TOK_DEV = 128
EXPERTS = 32
TOKENS = 4096
CAP = 40
HALF = 4
N_EXPERT = 8
N_DP = 4


def touch_ends(values, key, low, top_value):
    extent = values.shape
    index_at = [jax.random.randint(jax.random.fold_in(key, axis), (), 0, extent[axis]) for axis in range(len(extent))]
    values = values.at[tuple(index_at)].set(low)
    longest = extent.index(max(extent))
    index_at[longest] = (index_at[longest] + 1) % extent[longest]
    return values.at[tuple(index_at)].set(top_value)


def steps_of(rng, shape, shards, smallest, largest):
    def one(axis_at, blocks):
        heights = jax.random.uniform(jax.random.fold_in(jax.random.fold_in(rng, 6), axis_at), (blocks,), jnp.float32, smallest / len(shards), largest / len(shards))
        return jnp.repeat(jnp.exp(heights), shape[axis_at] // blocks).reshape((-1,) + (1,) * (len(shape) - axis_at - 1))

    factor_of = one(*shards[0])
    for cut in shards[1:]:
        factor_of = factor_of * one(*cut)
    return factor_of


def assign_block(stream_key, own, number, rows, amount, top, reach, slope):
    sequence = jax.random.permutation(stream_key, amount)
    packed, common = shares(amount, rows * top, reach, slope, True), shares(amount, rows * top, reach, slope, False)
    places = jnp.arange(amount)

    def named(sizes, rotation):
        used = int((sizes > 0).sum())
        fixed = max(1, used // 4)
        moved = fixed + (places - fixed + rotation * (used - fixed)) % max(1, amount - fixed)
        return jnp.zeros((amount,), jnp.int32).at[sequence[jnp.where(places < fixed, places, moved)]].set(jnp.asarray(sizes, jnp.int32))

    sizes = jnp.where(number % 4 == 0, named(packed, number // 4), named(common, number - number // 4 - 1))
    mixed = jax.random.permutation(jax.random.fold_in(own, 3), amount)
    source_of, taker = mixed[0:amount // 2 * 2:2], mixed[1:amount // 2 * 2:2]
    slack = jnp.minimum(sizes[source_of] - 1, reach - sizes[taker]) // 2
    slack = jnp.where((source_of == sequence[0]) | (taker == sequence[0]) | (sizes[taker] == 0), 0, jnp.maximum(slack, 0))
    moved = jax.random.randint(jax.random.fold_in(own, 4), (amount // 2,), 0, 1 << 20) % (slack + 1)
    sizes = sizes.at[source_of].add(-moved).at[taker].add(moved)
    members = jnp.searchsorted(jnp.cumsum(sizes), jnp.arange(rows * top), side="right").astype(jnp.int32)
    listing = members.reshape(top, rows).T
    listing = listing[jax.random.permutation(jax.random.fold_in(own, 1), rows)]
    rotation = jax.random.randint(jax.random.fold_in(own, 2), (rows, 1), 0, top)
    return jnp.take_along_axis(listing, (jnp.arange(top)[None, :] + rotation) % top, axis=1)


def shares(count, total, limit, slope, full):
    weights = [(1 << 20) // math.isqrt(rank ** slope) + 1 for rank in range(1, count + 1)]
    largest = limit if full else min(limit, max(-(-total // count), total * weights[0] // sum(weights)))
    least = 1 if total - largest >= count - 1 else 0
    holding, surplus = [largest] + [least] * (count - 1), total - largest - least * (count - 1)
    while surplus > 0:
        candidates = [i for i in range(1, count) if holding[i] < largest] or [i for i in range(1, count) if holding[i] < limit]
        mass, left = sum([weights[i] for i in candidates]), surplus
        for i in candidates:
            more = min(limit - holding[i], max(1, left * weights[i] // mass), surplus)
            holding[i] = holding[i] + more
            surplus = surplus - more
    return np.array(holding)


def centred(stream_key, shape, width, reach, split=(), kind=jnp.bfloat16):
    result = width * jax.random.normal(stream_key, shape, jnp.float32)
    if split:
        result = result * steps_of(stream_key, shape, split, -0.22, 0.18)
    return jnp.clip(result, -reach, reach).astype(kind)


def setup_inputs(seed: int = 0) -> dict:
    key_of = jax.random.split(jax.random.key(seed), 9)
    tokens = centred(key_of[0], (TOKENS, D), 1.0, 6.0, ((0, 32),))
    cotangent = centred(key_of[1], (TOKENS, D), 1.0, 6.0, ((0, 32),))
    expert_ids_keys = jax.random.split(jax.random.fold_in(key_of[2], 1), TOKENS // TOK_DEV)
    expert_ids_turns = jax.random.permutation(jax.random.fold_in(key_of[2], 3), TOKENS // TOK_DEV)
    expert_ids = jax.vmap(lambda own, number: assign_block(jax.random.fold_in(key_of[2], 2), own, number, TOK_DEV, EXPERTS, TOPK, CAP, 2))(expert_ids_keys, expert_ids_turns).reshape((TOKENS, TOPK))
    combine_weights = jnp.clip(jnp.exp(math.log(1.0) - 2.3025851 * jax.random.uniform(key_of[3], (TOKENS, TOPK), jnp.float32) ** steps_of(key_of[3], (TOKENS, TOPK), ((0, 32),), -0.2, 0.2)), 0.1, 1.0)
    w_gate = centred(key_of[4], (EXPERTS, D, FW), D ** -0.5, 0.125, ((0, 8),))
    w_up = centred(key_of[5], (EXPERTS, D, FW), D ** -0.5, 0.125, ((0, 8),))
    w_down = centred(key_of[6], (EXPERTS, D, FW), FW ** -0.5, 0.3125, ((0, 8),))
    swap_flags = touch_ends((jax.random.randint(key_of[7], (HALF,), 0, 2) < 1).astype(jnp.int32), jax.random.fold_in(key_of[7], 1), 0, 1)
    return dict(tokens=tokens, cotangent=cotangent, expert_ids=expert_ids, combine_weights=combine_weights, w_gate=w_gate, w_up=w_up, w_down=w_down, swap_flags=swap_flags)


def reference(tokens, cotangent, expert_ids, combine_weights, w_gate, w_up, w_down, swap_flags):
    route_count = TOKENS * TOPK
    flat_expert = expert_ids.reshape(route_count).astype(jnp.int32)
    route_token = jnp.arange(route_count, dtype=jnp.int32) // TOPK
    route_group = (route_token // TOK_DEV) % N_DP
    sort_keys = route_group * EXPERTS + flat_expert
    order = jnp.argsort(sort_keys, stable=True).astype(jnp.int32)
    sorted_keys = sort_keys[order]
    key_range = jnp.arange(N_DP * EXPERTS, dtype=jnp.int32)
    starts = jnp.searchsorted(sorted_keys, key_range, side="left").astype(jnp.int32)
    ends = jnp.searchsorted(sorted_keys, key_range, side="right").astype(jnp.int32)
    most_rows = N_EXPERT * CAP
    flat_weight = combine_weights.reshape(route_count)

    def per_expert(carry, expert):
        out_acc, grad_acc = carry
        gate_w = w_gate[expert]
        up_w = w_up[expert]
        down_w = w_down[expert]
        grad_sums = [jnp.zeros((D, FW), jnp.float32) for index in range(3)]
        for group in range(N_DP):
            key_now = group * EXPERTS + expert
            position = starts[key_now] + jnp.arange(most_rows, dtype=jnp.int32)
            valid = position < ends[key_now]
            route = order[jnp.minimum(position, route_count - 1)]
            token = route // TOPK
            rows = jnp.where(valid[:, None], tokens[token], jnp.zeros((), jnp.bfloat16))
            gate_pre = jnp.dot(rows, gate_w, preferred_element_type=jnp.float32)
            up_pre = jnp.dot(rows, up_w, preferred_element_type=jnp.float32)
            sigma = jax.nn.sigmoid(gate_pre)
            hidden = (gate_pre * sigma * up_pre).astype(jnp.bfloat16)
            expert_out = jnp.dot(hidden, down_w.T, preferred_element_type=jnp.float32).astype(jnp.bfloat16)
            weight_now = jnp.where(valid, flat_weight[route], jnp.zeros((), jnp.float32))
            out_acc = out_acc.at[token].add(weight_now[:, None] * expert_out.astype(jnp.float32))
            route_cot = (weight_now[:, None] * cotangent[token].astype(jnp.float32)).astype(jnp.bfloat16)
            hidden_cot = jnp.dot(route_cot, down_w, preferred_element_type=jnp.float32)
            gate_cot = (hidden_cot * up_pre * sigma * (1.0 + gate_pre * (1.0 - sigma))).astype(jnp.bfloat16)
            up_cot = (hidden_cot * gate_pre * sigma).astype(jnp.bfloat16)
            input_term = (jnp.dot(gate_cot, gate_w.T, preferred_element_type=jnp.float32)
                          + jnp.dot(up_cot, up_w.T, preferred_element_type=jnp.float32)).astype(jnp.bfloat16)
            grad_acc = grad_acc.at[token].add(jnp.where(valid[:, None], input_term.astype(jnp.float32), jnp.zeros((), jnp.float32)))
            partials = (jnp.dot(rows.T, gate_cot, preferred_element_type=jnp.float32),
                        jnp.dot(rows.T, up_cot, preferred_element_type=jnp.float32),
                        jnp.dot(route_cot.T, hidden, preferred_element_type=jnp.float32))
            for index in range(3):
                rounded = lax.optimization_barrier(partials[index].astype(jnp.bfloat16))
                grad_sums[index] = grad_sums[index] + rounded.astype(jnp.float32)
        return (out_acc, grad_acc), tuple(total.astype(jnp.bfloat16) for total in grad_sums)

    start_carry = (jnp.zeros((TOKENS, D), jnp.float32), jnp.zeros((TOKENS, D), jnp.float32))
    (out_acc, grad_acc), grads = lax.scan(per_expert, start_carry, jnp.arange(EXPERTS, dtype=jnp.int32))
    places = jnp.arange(EXPERTS, dtype=jnp.int32)
    holder = places // EXP_DEV
    position_in = places % EXP_DEV
    flagged = swap_flags[holder % HALF] == 1
    moved = flagged & (position_in == EXP_DEV - 1)
    source = jnp.where(moved, ((holder + HALF) % N_EXPERT) * EXP_DEV + position_in, places).astype(jnp.int32)
    return (out_acc.astype(jnp.bfloat16), grad_acc.astype(jnp.bfloat16),
            grads[0][source], grads[1][source], grads[2][source])
```

```python
import jax
import jax.numpy as jnp
from jax import lax
from jax.experimental import pallas as pl
from jax.experimental.pallas import tpu as pltpu
from jax.sharding import PartitionSpec as P

F32 = jnp.float32
BF16 = jnp.bfloat16
VMEM_BYTES = 56 * 1024 * 1024


def dot(a, b, dims):
    return lax.dot_general(a, b, (dims, ((), ())), preferred_element_type=F32)


def forward_kernel(slot_ref, x_ref, wg_ref, wu_ref, wd_ref, out_ref, hid_ref, dgate_ref, dup_ref):
    x = x_ref[...]
    gate = dot(x, wg_ref[...], ((1,), (0,)))
    up = dot(x, wu_ref[...], ((1,), (0,)))
    s = jax.nn.sigmoid(gate)
    silu = gate * s
    hidden = (silu * up).astype(BF16)
    hid_ref[...] = hidden
    dgate_ref[...] = up * s * (1.0 + gate * (1.0 - s))
    dup_ref[...] = silu
    out_ref[...] = dot(hidden, wd_ref[...], ((1,), (1,))).astype(BF16)


def backward_kernel(
    slot_ref, c_ref, dgate_ref, dup_ref, wg_ref, wu_ref, wd_ref, term_ref, gc_ref, uc_ref
):
    hidden_cot = dot(c_ref[...], wd_ref[...], ((1,), (0,)))
    gate_cot = (hidden_cot * dgate_ref[...]).astype(BF16)
    up_cot = (hidden_cot * dup_ref[...]).astype(BF16)
    gc_ref[...] = gate_cot
    uc_ref[...] = up_cot
    term_ref[...] = (
        dot(gate_cot, wg_ref[...], ((1,), (1,))) + dot(up_cot, wu_ref[...], ((1,), (1,)))
    ).astype(BF16)


def grads_kernel(x_ref, c_ref, gc_ref, uc_ref, hid_ref, out_ref):
    x = x_ref[...]
    out_ref[0, 0] = dot(x, gc_ref[...], ((0,), (0,))).astype(BF16)
    out_ref[0, 1] = dot(x, uc_ref[...], ((0,), (0,))).astype(BF16)
    out_ref[0, 2] = dot(c_ref[...], hid_ref[...], ((0,), (0,))).astype(BF16)


def expert_forward(slot, x, w_gate, w_up, w_down):
    rows, width = x.shape
    feat = w_gate.shape[2]
    tile = rows // 4
    weight = pl.BlockSpec((None, width, feat), lambda i, s: (s[0], 0, 0))
    wide = pl.BlockSpec((tile, width), lambda i, s: (i, 0))
    thin = pl.BlockSpec((tile, feat), lambda i, s: (i, 0))
    return pl.pallas_call(
        forward_kernel,
        grid_spec=pltpu.PrefetchScalarGridSpec(
            num_scalar_prefetch=1,
            grid=(rows // tile,),
            in_specs=[wide, weight, weight, weight],
            out_specs=[wide, thin, thin, thin],
        ),
        out_shape=[
            jax.ShapeDtypeStruct((rows, width), BF16),
            jax.ShapeDtypeStruct((rows, feat), BF16),
            jax.ShapeDtypeStruct((rows, feat), F32),
            jax.ShapeDtypeStruct((rows, feat), F32),
        ],
        compiler_params=pltpu.CompilerParams(vmem_limit_bytes=VMEM_BYTES),
        cost_estimate=pl.CostEstimate(
            flops=6 * rows * width * feat,
            bytes_accessed=4 * rows * width + 6 * width * feat + 10 * rows * feat,
            transcendentals=rows * feat,
        ),
    )(slot, x, w_gate, w_up, w_down)


def expert_backward(slot, c, dgate, dup, w_gate, w_up, w_down):
    rows, width = c.shape
    feat = w_gate.shape[2]
    tile = rows // 4
    weight = pl.BlockSpec((None, width, feat), lambda i, s: (s[0], 0, 0))
    wide = pl.BlockSpec((tile, width), lambda i, s: (i, 0))
    thin = pl.BlockSpec((tile, feat), lambda i, s: (i, 0))
    return pl.pallas_call(
        backward_kernel,
        grid_spec=pltpu.PrefetchScalarGridSpec(
            num_scalar_prefetch=1,
            grid=(rows // tile,),
            in_specs=[wide, thin, thin, weight, weight, weight],
            out_specs=[wide, thin, thin],
        ),
        out_shape=[
            jax.ShapeDtypeStruct((rows, width), BF16),
            jax.ShapeDtypeStruct((rows, feat), BF16),
            jax.ShapeDtypeStruct((rows, feat), BF16),
        ],
        compiler_params=pltpu.CompilerParams(vmem_limit_bytes=VMEM_BYTES),
        cost_estimate=pl.CostEstimate(
            flops=6 * rows * width * feat,
            bytes_accessed=4 * rows * width + 6 * width * feat + 12 * rows * feat,
            transcendentals=0,
        ),
    )(slot, c, dgate, dup, w_gate, w_up, w_down)


def expert_grads(x, c, gate_cot, up_cot, hidden, parts):
    rows, width = x.shape
    feat = hidden.shape[1]
    cols = width // parts
    wide = pl.BlockSpec((rows, cols), lambda i: (0, i))
    thin = pl.BlockSpec((rows, feat), lambda i: (0, 0))
    return pl.pallas_call(
        grads_kernel,
        grid=(parts,),
        in_specs=[wide, wide, thin, thin, thin],
        out_specs=pl.BlockSpec((1, 3, cols, feat), lambda i: (i, 0, 0, 0)),
        out_shape=jax.ShapeDtypeStruct((parts, 3, cols, feat), BF16),
        compiler_params=pltpu.CompilerParams(vmem_limit_bytes=VMEM_BYTES),
        cost_estimate=pl.CostEstimate(
            flops=6 * rows * width * feat,
            bytes_accessed=4 * rows * width + 6 * width * feat + 6 * rows * feat,
            transcendentals=0,
        ),
    )(x, c, gate_cot, up_cot, hidden)


def local(tokens, cotangent, expert_ids, combine_weights, w_gate, w_up, w_down, swap_flags):
    tok_rows, width = tokens.shape
    top_count = expert_ids.shape[1]
    per_device = w_gate.shape[0]
    groups = lax.axis_size("expert")
    parts = lax.axis_size("dp")
    half = groups // 2
    experts_all = groups * per_device
    capacity = tok_rows * top_count * 5 // (4 * experts_all) * parts
    total = groups * capacity
    mine = lax.axis_index("dp")
    slot = mine.astype(jnp.int32).reshape(1)

    info = jnp.concatenate([expert_ids.astype(F32), combine_weights], axis=1)
    info = lax.all_gather(info, "dp", tiled=True)
    tok_all = lax.all_gather(tokens, "dp", tiled=True)
    cot_all = lax.all_gather(cotangent, "dp", tiled=True)
    ids = info[:, :top_count].astype(jnp.int32)
    weights = info[:, top_count:]
    count = ids.shape[0]
    wanted = jnp.arange(groups, dtype=jnp.int32) * per_device + mine
    match = ids[:, :, None] == wanted[None, None, :]
    hit = jnp.any(match, axis=1)
    route_weight = jnp.sum(jnp.where(match, weights[:, :, None], 0.0), axis=1)
    below = (jnp.arange(count)[:, None] > jnp.arange(count)[None, :]).astype(BF16)
    rank = dot(below, hit.astype(BF16), ((1,), (0,))).astype(jnp.int32)
    place = jnp.where(hit, rank, -1).T
    picked = place[:, None, :] == jnp.arange(capacity, dtype=jnp.int32)[None, :, None]
    row_weight = jnp.sum(jnp.where(picked, route_weight.T[:, None, :], 0.0), axis=2).reshape(total, 1)
    pick = picked.astype(BF16).reshape(total, count)
    pick_weighted = (
        jnp.where(picked, route_weight.T[:, None, :], 0.0).astype(BF16).reshape(total, count)
    )

    def exchange(value):
        shape = (groups, capacity, width)
        return lax.all_to_all(
            value.reshape(shape), "expert", split_axis=0, concat_axis=0, tiled=True
        ).reshape(total, width)

    x = exchange(dot(pick, tok_all, ((1,), (0,))).astype(BF16))
    c = exchange((dot(pick, cot_all, ((1,), (0,))) * row_weight).astype(BF16))
    out, hidden, dgate, dup = expert_forward(slot, x, w_gate, w_up, w_down)
    out_back = exchange(out)
    term, gate_cot, up_cot = expert_backward(slot, c, dgate, dup, w_gate, w_up, w_down)
    grads = expert_grads(x, c, gate_cot, up_cot, hidden, parts)
    grads = lax.all_to_all(grads, "dp", split_axis=0, concat_axis=0, tiled=True)
    term_back = exchange(term)

    mixed_part = dot(pick_weighted, out_back, ((0,), (0,))).astype(BF16)
    mixed = lax.psum_scatter(mixed_part, "dp", scatter_dimension=0, tiled=True)
    input_part = dot(pick, term_back, ((0,), (0,))).astype(BF16)
    input_grad = lax.psum_scatter(input_part, "dp", scatter_dimension=0, tiled=True)

    last = grads[per_device - 1]
    pairs = [(i, (i + half) % groups) for i in range(groups)]
    peer = lax.ppermute(last, "expert", pairs)
    pair = lax.axis_index("expert") % half
    flag = jnp.sum(jnp.where(jnp.arange(half) == pair, swap_flags, 0)) == 1
    chosen = jnp.where(flag, peer, last)
    out_grads = [
        jnp.concatenate([grads[: per_device - 1, m], chosen[None, m]], axis=0) for m in range(3)
    ]
    return (mixed, input_grad, *out_grads)


def solution(mesh):
    return jax.shard_map(
        local,
        mesh=mesh,
        in_specs=(
            P(("expert", "dp"), None),
            P(("expert", "dp"), None),
            P(("expert", "dp"), None),
            P(("expert", "dp"), None),
            P("expert", None, None),
            P("expert", None, None),
            P("expert", None, None),
            P(),
        ),
        out_specs=(
            P(("expert", "dp"), None),
            P(("expert", "dp"), None),
            P("expert", "dp", None),
            P("expert", "dp", None),
            P("expert", "dp", None),
        ),
        check_vma=False,
    )
```

```python
import jax
import jax.numpy as jnp
from jax import lax
from jax.experimental import pallas as pl
from jax.experimental.pallas import tpu as pltpu
from jax.sharding import PartitionSpec as P

F32 = jnp.float32
BF16 = jnp.bfloat16
VMEM_BYTES = 56 * 1024 * 1024


def dot(a, b, dims):
    return lax.dot_general(a, b, (dims, ((), ())), preferred_element_type=F32)


def forward_kernel(slot_ref, x_ref, wg_ref, wu_ref, wd_ref, out_ref, hid_ref, dgate_ref, dup_ref):
    x = x_ref[...]
    gate = dot(x, wg_ref[...], ((1,), (0,)))
    up = dot(x, wu_ref[...], ((1,), (0,)))
    s = jax.nn.sigmoid(gate)
    silu = gate * s
    hidden = (silu * up).astype(BF16)
    hid_ref[...] = hidden
    dgate_ref[...] = up * s * (1.0 + gate * (1.0 - s))
    dup_ref[...] = silu
    out_ref[...] = dot(hidden, wd_ref[...], ((1,), (1,))).astype(BF16)


def backward_kernel(
    slot_ref, c_ref, dgate_ref, dup_ref, wg_ref, wu_ref, wd_ref, term_ref, gc_ref, uc_ref
):
    hidden_cot = dot(c_ref[...], wd_ref[...], ((1,), (0,)))
    gate_cot = (hidden_cot * dgate_ref[...]).astype(BF16)
    up_cot = (hidden_cot * dup_ref[...]).astype(BF16)
    gc_ref[...] = gate_cot
    uc_ref[...] = up_cot
    term_ref[...] = (
        dot(gate_cot, wg_ref[...], ((1,), (1,))) + dot(up_cot, wu_ref[...], ((1,), (1,)))
    ).astype(BF16)


def grads_kernel(x_ref, c_ref, gc_ref, uc_ref, hid_ref, out_ref):
    x = x_ref[...]
    out_ref[0, 0] = dot(x, gc_ref[...], ((0,), (0,))).astype(BF16)
    out_ref[0, 1] = dot(x, uc_ref[...], ((0,), (0,))).astype(BF16)
    out_ref[0, 2] = dot(c_ref[...], hid_ref[...], ((0,), (0,))).astype(BF16)


def expert_forward(slot, x, w_gate, w_up, w_down):
    rows, width = x.shape
    feat = w_gate.shape[2]
    tile = rows // 4
    weight = pl.BlockSpec((None, width, feat), lambda i, s: (s[0], 0, 0))
    wide = pl.BlockSpec((tile, width), lambda i, s: (i, 0))
    thin = pl.BlockSpec((tile, feat), lambda i, s: (i, 0))
    return pl.pallas_call(
        forward_kernel,
        grid_spec=pltpu.PrefetchScalarGridSpec(
            num_scalar_prefetch=1,
            grid=(rows // tile,),
            in_specs=[wide, weight, weight, weight],
            out_specs=[wide, thin, thin, thin],
        ),
        out_shape=[
            jax.ShapeDtypeStruct((rows, width), BF16),
            jax.ShapeDtypeStruct((rows, feat), BF16),
            jax.ShapeDtypeStruct((rows, feat), F32),
            jax.ShapeDtypeStruct((rows, feat), F32),
        ],
        compiler_params=pltpu.CompilerParams(vmem_limit_bytes=VMEM_BYTES),
        cost_estimate=pl.CostEstimate(
            flops=6 * rows * width * feat,
            bytes_accessed=4 * rows * width + 6 * width * feat + 10 * rows * feat,
            transcendentals=rows * feat,
        ),
    )(slot, x, w_gate, w_up, w_down)


def expert_backward(slot, c, dgate, dup, w_gate, w_up, w_down):
    rows, width = c.shape
    feat = w_gate.shape[2]
    tile = rows // 4
    weight = pl.BlockSpec((None, width, feat), lambda i, s: (s[0], 0, 0))
    wide = pl.BlockSpec((tile, width), lambda i, s: (i, 0))
    thin = pl.BlockSpec((tile, feat), lambda i, s: (i, 0))
    return pl.pallas_call(
        backward_kernel,
        grid_spec=pltpu.PrefetchScalarGridSpec(
            num_scalar_prefetch=1,
            grid=(rows // tile,),
            in_specs=[wide, thin, thin, weight, weight, weight],
            out_specs=[wide, thin, thin],
        ),
        out_shape=[
            jax.ShapeDtypeStruct((rows, width), BF16),
            jax.ShapeDtypeStruct((rows, feat), BF16),
            jax.ShapeDtypeStruct((rows, feat), BF16),
        ],
        compiler_params=pltpu.CompilerParams(vmem_limit_bytes=VMEM_BYTES),
        cost_estimate=pl.CostEstimate(
            flops=6 * rows * width * feat,
            bytes_accessed=4 * rows * width + 6 * width * feat + 12 * rows * feat,
            transcendentals=0,
        ),
    )(slot, c, dgate, dup, w_gate, w_up, w_down)


def expert_grads(x, c, gate_cot, up_cot, hidden, parts):
    rows, width = x.shape
    feat = hidden.shape[1]
    cols = width // parts
    wide = pl.BlockSpec((rows, cols), lambda i: (0, i))
    thin = pl.BlockSpec((rows, feat), lambda i: (0, 0))
    return pl.pallas_call(
        grads_kernel,
        grid=(parts,),
        in_specs=[wide, wide, thin, thin, thin],
        out_specs=pl.BlockSpec((1, 3, cols, feat), lambda i: (i, 0, 0, 0)),
        out_shape=jax.ShapeDtypeStruct((parts, 3, cols, feat), BF16),
        compiler_params=pltpu.CompilerParams(vmem_limit_bytes=VMEM_BYTES),
        cost_estimate=pl.CostEstimate(
            flops=6 * rows * width * feat,
            bytes_accessed=4 * rows * width + 6 * width * feat + 6 * rows * feat,
            transcendentals=0,
        ),
    )(x, c, gate_cot, up_cot, hidden)


def local(tokens, cotangent, expert_ids, combine_weights, w_gate, w_up, w_down, swap_flags):
    tok_rows, width = tokens.shape
    top_count = expert_ids.shape[1]
    per_device = w_gate.shape[0]
    groups = lax.axis_size("expert")
    parts = lax.axis_size("dp")
    half = groups // 2
    experts_all = groups * per_device
    capacity = tok_rows * top_count * 5 // (4 * experts_all) * parts
    total = groups * capacity
    mine = lax.axis_index("dp")
    slot = mine.astype(jnp.int32).reshape(1)

    info = jnp.concatenate([expert_ids.astype(F32), combine_weights], axis=1)
    info = lax.all_gather(info, "dp", tiled=True)
    tok_all = lax.all_gather(tokens, "dp", tiled=True)
    cot_all = lax.all_gather(cotangent, "dp", tiled=True)
    ids = info[:, :top_count].astype(jnp.int32)
    weights = info[:, top_count:]
    count = ids.shape[0]
    wanted = jnp.arange(groups, dtype=jnp.int32) * per_device + mine
    match = ids[:, :, None] == wanted[None, None, :]
    hit = jnp.any(match, axis=1)
    route_weight = jnp.sum(jnp.where(match, weights[:, :, None], 0.0), axis=1)
    below = (jnp.arange(count)[:, None] > jnp.arange(count)[None, :]).astype(BF16)
    rank = dot(below, hit.astype(BF16), ((1,), (0,))).astype(jnp.int32)
    place = jnp.where(hit, rank, -1).T
    picked = place[:, None, :] == jnp.arange(capacity, dtype=jnp.int32)[None, :, None]
    row_weight = jnp.sum(jnp.where(picked, route_weight.T[:, None, :], 0.0), axis=2).reshape(total, 1)
    pick = picked.astype(BF16).reshape(total, count)
    pick_weighted = (
        jnp.where(picked, route_weight.T[:, None, :], 0.0).astype(BF16).reshape(total, count)
    )

    def exchange(value):
        shape = (groups, capacity, width)
        return lax.all_to_all(
            value.reshape(shape), "expert", split_axis=0, concat_axis=0, tiled=True
        ).reshape(total, width)

    x = exchange(dot(pick, tok_all, ((1,), (0,))).astype(BF16))
    c = exchange((dot(pick, cot_all, ((1,), (0,))) * row_weight).astype(BF16))
    out, hidden, dgate, dup = expert_forward(slot, x, w_gate, w_up, w_down)
    out_back = exchange(out)
    term, gate_cot, up_cot = expert_backward(slot, c, dgate, dup, w_gate, w_up, w_down)
    grads = expert_grads(x, c, gate_cot, up_cot, hidden, parts)
    term, grads = lax.optimization_barrier((term, grads))
    received = [lax.dynamic_index_in_dim(grads, mine, keepdims=False)]
    for step in range(1, parts):
        sent = lax.dynamic_index_in_dim(grads, mine ^ step, keepdims=False)
        received.append(lax.ppermute(sent, "dp", [(i, i ^ step) for i in range(parts)]))
    term, *early = lax.optimization_barrier((term, *received[:-1]))
    term_back = exchange(term)
    term_back, final = lax.optimization_barrier((term_back, received[-1]))
    received = [*early, final]

    mixed_part = dot(pick_weighted, out_back, ((0,), (0,))).astype(BF16)
    mixed = lax.psum_scatter(mixed_part, "dp", scatter_dimension=0, tiled=True)
    input_part = dot(pick, term_back, ((0,), (0,))).astype(BF16)
    input_grad = lax.psum_scatter(input_part, "dp", scatter_dimension=0, tiled=True)

    last = lax.select_n((per_device - 1) ^ mine, *received)
    pairs = [(i, (i + half) % groups) for i in range(groups)]
    peer = lax.ppermute(last, "expert", pairs)
    pair = lax.axis_index("expert") % half
    flag = jnp.sum(jnp.where(jnp.arange(half) == pair, swap_flags, 0)) == 1
    chosen = jnp.where(flag, peer, last)
    out_grads = []
    for m in range(3):
        whole = jnp.zeros((per_device,) + last.shape[1:], BF16)
        for step in range(parts):
            whole = lax.dynamic_update_index_in_dim(whole, received[step][m], mine ^ step, 0)
        out_grads.append(whole.at[per_device - 1].set(chosen[m]))
    return (mixed, input_grad, *out_grads)


def solution(mesh):
    return jax.shard_map(
        local,
        mesh=mesh,
        in_specs=(
            P(("expert", "dp"), None),
            P(("expert", "dp"), None),
            P(("expert", "dp"), None),
            P(("expert", "dp"), None),
            P("expert", None, None),
            P("expert", None, None),
            P("expert", None, None),
            P(),
        ),
        out_specs=(
            P(("expert", "dp"), None),
            P(("expert", "dp"), None),
            P("expert", "dp", None),
            P("expert", "dp", None),
            P("expert", "dp", None),
        ),
        check_vma=False,
    )
```

```python
import jax
import jax.numpy as jnp
from jax import lax
from jax.experimental import pallas as pl
from jax.experimental.pallas import tpu as pltpu
from jax.sharding import PartitionSpec as P

F32 = jnp.float32
BF16 = jnp.bfloat16
VMEM_BYTES = 56 * 1024 * 1024


def dot(a, b, dims):
    return lax.dot_general(a, b, (dims, ((), ())), preferred_element_type=F32)


def forward_kernel(slot_ref, x_ref, wg_ref, wu_ref, wd_ref, out_ref, hid_ref, dgate_ref, dup_ref):
    x = x_ref[...]
    gate = dot(x, wg_ref[...], ((1,), (0,)))
    up = dot(x, wu_ref[...], ((1,), (0,)))
    s = jax.nn.sigmoid(gate)
    silu = gate * s
    hidden = (silu * up).astype(BF16)
    hid_ref[...] = hidden
    dgate_ref[...] = up * s * (1.0 + gate * (1.0 - s))
    dup_ref[...] = silu
    out_ref[...] = dot(hidden, wd_ref[...], ((1,), (1,))).astype(BF16)


def backward_kernel(
    slot_ref, c_ref, dgate_ref, dup_ref, wg_ref, wu_ref, wd_ref, term_ref, gc_ref, uc_ref
):
    hidden_cot = dot(c_ref[...], wd_ref[...], ((1,), (0,)))
    gate_cot = (hidden_cot * dgate_ref[...]).astype(BF16)
    up_cot = (hidden_cot * dup_ref[...]).astype(BF16)
    gc_ref[...] = gate_cot
    uc_ref[...] = up_cot
    term_ref[...] = (
        dot(gate_cot, wg_ref[...], ((1,), (1,))) + dot(up_cot, wu_ref[...], ((1,), (1,)))
    ).astype(BF16)


def grads_kernel(lhs_ref, *refs):
    lhs = lhs_ref[...]
    out_ref = refs[-1]
    for k, right_ref in enumerate(refs[:-1]):
        out_ref[0, k] = dot(lhs, right_ref[...], ((0,), (0,))).astype(BF16)


def expert_forward(slot, x, w_gate, w_up, w_down):
    rows, width = x.shape
    feat = w_gate.shape[2]
    tile = rows // 4
    weight = pl.BlockSpec((None, width, feat), lambda i, s: (s[0], 0, 0))
    wide = pl.BlockSpec((tile, width), lambda i, s: (i, 0))
    thin = pl.BlockSpec((tile, feat), lambda i, s: (i, 0))
    return pl.pallas_call(
        forward_kernel,
        grid_spec=pltpu.PrefetchScalarGridSpec(
            num_scalar_prefetch=1,
            grid=(rows // tile,),
            in_specs=[wide, weight, weight, weight],
            out_specs=[wide, thin, thin, thin],
        ),
        out_shape=[
            jax.ShapeDtypeStruct((rows, width), BF16),
            jax.ShapeDtypeStruct((rows, feat), BF16),
            jax.ShapeDtypeStruct((rows, feat), F32),
            jax.ShapeDtypeStruct((rows, feat), F32),
        ],
        compiler_params=pltpu.CompilerParams(vmem_limit_bytes=VMEM_BYTES),
        cost_estimate=pl.CostEstimate(
            flops=6 * rows * width * feat,
            bytes_accessed=4 * rows * width + 6 * width * feat + 10 * rows * feat,
            transcendentals=rows * feat,
        ),
    )(slot, x, w_gate, w_up, w_down)


def expert_backward(slot, c, dgate, dup, w_gate, w_up, w_down):
    rows, width = c.shape
    feat = w_gate.shape[2]
    tile = rows // 4
    weight = pl.BlockSpec((None, width, feat), lambda i, s: (s[0], 0, 0))
    wide = pl.BlockSpec((tile, width), lambda i, s: (i, 0))
    thin = pl.BlockSpec((tile, feat), lambda i, s: (i, 0))
    return pl.pallas_call(
        backward_kernel,
        grid_spec=pltpu.PrefetchScalarGridSpec(
            num_scalar_prefetch=1,
            grid=(rows // tile,),
            in_specs=[wide, thin, thin, weight, weight, weight],
            out_specs=[wide, thin, thin],
        ),
        out_shape=[
            jax.ShapeDtypeStruct((rows, width), BF16),
            jax.ShapeDtypeStruct((rows, feat), BF16),
            jax.ShapeDtypeStruct((rows, feat), BF16),
        ],
        compiler_params=pltpu.CompilerParams(vmem_limit_bytes=VMEM_BYTES),
        cost_estimate=pl.CostEstimate(
            flops=6 * rows * width * feat,
            bytes_accessed=4 * rows * width + 6 * width * feat + 12 * rows * feat,
            transcendentals=0,
        ),
    )(slot, c, dgate, dup, w_gate, w_up, w_down)


def expert_grads(lhs, rights, parts):
    rows, width = lhs.shape
    feat = rights[0].shape[1]
    number = len(rights)
    cols = width // parts
    thin = pl.BlockSpec((rows, feat), lambda i: (0, 0))
    return pl.pallas_call(
        grads_kernel,
        grid=(parts,),
        in_specs=[pl.BlockSpec((rows, cols), lambda i: (0, i))] + [thin] * number,
        out_specs=pl.BlockSpec((1, number, cols, feat), lambda i: (i, 0, 0, 0)),
        out_shape=jax.ShapeDtypeStruct((parts, number, cols, feat), BF16),
        compiler_params=pltpu.CompilerParams(vmem_limit_bytes=VMEM_BYTES),
        cost_estimate=pl.CostEstimate(
            flops=2 * number * rows * width * feat,
            bytes_accessed=2 * rows * width + 2 * number * (width + rows) * feat,
            transcendentals=0,
        ),
    )(lhs, *rights)


def local(tokens, cotangent, expert_ids, combine_weights, w_gate, w_up, w_down, swap_flags):
    tok_rows, width = tokens.shape
    top_count = expert_ids.shape[1]
    per_device = w_gate.shape[0]
    groups = lax.axis_size("expert")
    parts = lax.axis_size("dp")
    half = groups // 2
    experts_all = groups * per_device
    capacity = tok_rows * top_count * 5 // (4 * experts_all) * parts
    total = groups * capacity
    mine = lax.axis_index("dp")
    slot = mine.astype(jnp.int32).reshape(1)

    info = jnp.concatenate([expert_ids.astype(F32), combine_weights], axis=1)
    info = lax.all_gather(info, "dp", tiled=True)
    tok_all = lax.all_gather(tokens, "dp", tiled=True)
    cot_all = lax.all_gather(cotangent, "dp", tiled=True)
    ids = info[:, :top_count].astype(jnp.int32)
    weights = info[:, top_count:]
    count = ids.shape[0]
    wanted = jnp.arange(groups, dtype=jnp.int32) * per_device + mine
    match = ids[:, :, None] == wanted[None, None, :]
    hit = jnp.any(match, axis=1)
    route_weight = jnp.sum(jnp.where(match, weights[:, :, None], 0.0), axis=1)
    below = (jnp.arange(count)[:, None] > jnp.arange(count)[None, :]).astype(BF16)
    rank = dot(below, hit.astype(BF16), ((1,), (0,))).astype(jnp.int32)
    place = jnp.where(hit, rank, -1).T
    picked = place[:, None, :] == jnp.arange(capacity, dtype=jnp.int32)[None, :, None]
    row_weight = jnp.sum(jnp.where(picked, route_weight.T[:, None, :], 0.0), axis=2).reshape(total, 1)
    pick = picked.astype(BF16).reshape(total, count)
    pick_weighted = (
        jnp.where(picked, route_weight.T[:, None, :], 0.0).astype(BF16).reshape(total, count)
    )

    def exchange(value):
        shape = (groups, capacity, width)
        return lax.all_to_all(
            value.reshape(shape), "expert", split_axis=0, concat_axis=0, tiled=True
        ).reshape(total, width)

    x = exchange(dot(pick, tok_all, ((1,), (0,))).astype(BF16))
    c = exchange((dot(pick, cot_all, ((1,), (0,))) * row_weight).astype(BF16))
    out, hidden, dgate, dup = expert_forward(slot, x, w_gate, w_up, w_down)
    out_back = exchange(out)

    def blocks(grads):
        return [
            lax.dynamic_index_in_dim(grads, mine ^ step, keepdims=False) for step in range(parts)
        ]

    def swap(block, step):
        return lax.ppermute(block, "dp", [(i, i ^ step) for i in range(parts)])

    down = blocks(expert_grads(c, [hidden], parts))
    dgate, *down = lax.optimization_barrier((dgate, *down))
    down = down[:1] + [swap(down[step], step) for step in range(1, parts)]
    term, gate_cot, up_cot = expert_backward(slot, c, dgate, dup, w_gate, w_up, w_down)
    both = blocks(expert_grads(x, [gate_cot, up_cot], parts))
    both[0], *moved = lax.optimization_barrier((both[0], *both[1:], *down[1:]))
    both, down = both[:1] + moved[: parts - 1], down[:1] + moved[parts - 1 :]
    both = both[:1] + [swap(both[step], step) for step in range(1, parts)]
    term, *ready = lax.optimization_barrier((term, *down, *both[:-1]))
    term_back = exchange(term)
    term_back, final = lax.optimization_barrier((term_back, both[-1]))
    down, both = ready[:parts], [*ready[parts:], final]
    received = [jnp.concatenate([b, d], axis=0) for b, d in zip(both, down)]

    mixed_part = dot(pick_weighted, out_back, ((0,), (0,))).astype(BF16)
    mixed = lax.psum_scatter(mixed_part, "dp", scatter_dimension=0, tiled=True)
    input_part = dot(pick, term_back, ((0,), (0,))).astype(BF16)
    input_grad = lax.psum_scatter(input_part, "dp", scatter_dimension=0, tiled=True)

    last = lax.select_n((per_device - 1) ^ mine, *received)
    pairs = [(i, (i + half) % groups) for i in range(groups)]
    peer = lax.ppermute(last, "expert", pairs)
    pair = lax.axis_index("expert") % half
    flag = jnp.sum(jnp.where(jnp.arange(half) == pair, swap_flags, 0)) == 1
    chosen = jnp.where(flag, peer, last)
    out_grads = []
    for m in range(3):
        whole = jnp.zeros((per_device,) + last.shape[1:], BF16)
        for step in range(parts):
            whole = lax.dynamic_update_index_in_dim(whole, received[step][m], mine ^ step, 0)
        out_grads.append(whole.at[per_device - 1].set(chosen[m]))
    return (mixed, input_grad, *out_grads)


def solution(mesh):
    return jax.shard_map(
        local,
        mesh=mesh,
        in_specs=(
            P(("expert", "dp"), None),
            P(("expert", "dp"), None),
            P(("expert", "dp"), None),
            P(("expert", "dp"), None),
            P("expert", None, None),
            P("expert", None, None),
            P("expert", None, None),
            P(),
        ),
        out_specs=(
            P(("expert", "dp"), None),
            P(("expert", "dp"), None),
            P("expert", "dp", None),
            P("expert", "dp", None),
            P("expert", "dp", None),
        ),
        check_vma=False,
    )
```
